32 devices in a mesh: tile: 8 (over y, x, core), col: 4 (over z).
Axes of the slice: x: 2, y: 2, z: 4, core: 2. Of those that a mesh axis runs over, the one named last changes fastest.
Arguments:
- impedance: bfloat16 [2, 16384, 16384], P(None, 'tile', 'col'), may hold values from -0.0234375 to 0.0234375
- mobility: bfloat16 [256, 64, 128], P('tile'), may hold values from -0.5 to 0.5
- force: bfloat16 [512, 256, 128], P('col', 'tile'), may hold values from -6 to 6
- patch_map: int32 [16384], replicated, may hold values from 0 to 16383, each once
- ownership: int32 [256], P('tile'), may hold values from 0 to 255, each once
Outputs:
- velocity: bfloat16 [512, 256, 128], P('col', 'tile')
- pressure: bfloat16 [512, 2, 16384], P('col', None, 'tile')
The draws below stay inside these ranges and needn't reach their ends.
Inputs may be any that keep to these rules, and one draw needn't show every extreme that they name: `patch_map`: each patch appears exactly once. `ownership`: each panel appears exactly once.
All inputs are finite; a program needn't handle non-finite values.
Results may differ from the reference program's by a relative error of at most 0.018.
Values may be sent and summed in bfloat16 or wider, within the bound.
A program may use at most 128 MiB of HBM per device.

```python
import jax
import jax.numpy as jnp
from jax import lax

P_SIZE = 16384
K = 64
LOADS = 512
ITERS = 2
PANELS = 256


def level_of(own_key, extent, cuts, smallest, high):
    def one(dim, blocks):
        steps = jax.random.uniform(jax.random.fold_in(jax.random.fold_in(own_key, 6), dim), (blocks,), jnp.float32, smallest / len(cuts), high / len(cuts))
        return jnp.repeat(jnp.exp(steps), extent[dim] // blocks).reshape((-1,) + (1,) * (len(extent) - dim - 1))

    factor_of = one(*cuts[0])
    for cut in cuts[1:]:
        factor_of = factor_of * one(*cut)
    return factor_of


def centred(own_key, shape, width, most, cuts=(), held_as=jnp.bfloat16):
    level = level_of(own_key, shape, cuts, -0.22, 0.18) if cuts else 1.0
    entries = jax.random.normal(own_key, shape, jnp.float32) * width * level
    return jnp.minimum(jnp.maximum(entries, -most), most).astype(held_as)


def setup_inputs(seed: int = 0) -> dict:
    key_list = jax.random.split(jax.random.key(seed), 6)
    return {
        "impedance": centred(key_list[0], (2, P_SIZE, P_SIZE), (4 * P_SIZE) ** -0.5, 0.0234375, ((1, 8), (2, 4))),
        "mobility": centred(key_list[1], (PANELS, K, 2 * K), (2 * K) ** -0.5, 0.5, ((0, 8),)),
        "force": centred(key_list[2], (LOADS, PANELS, 2 * K), 1.0, 6.0, ((0, 4), (1, 8))),
        "patch_map": jax.random.permutation(key_list[3], P_SIZE).astype(jnp.int32),
        "ownership": jax.random.permutation(key_list[4], PANELS).astype(jnp.int32),
    }


def impedance_product(impedance, field):
    highest = lax.Precision.HIGHEST
    vel_re = field[:, 0].astype(jnp.float32)
    vel_im = field[:, 1].astype(jnp.float32)
    rows_block = P_SIZE // 16

    def one_block(block_index):
        z_block = lax.dynamic_slice_in_dim(impedance, block_index * rows_block, rows_block, 1).astype(jnp.float32)
        real_part = jnp.dot(vel_re, z_block[0].T, precision=highest) - jnp.dot(vel_im, z_block[1].T, precision=highest)
        imag_part = jnp.dot(vel_re, z_block[1].T, precision=highest) + jnp.dot(vel_im, z_block[0].T, precision=highest)
        return jnp.stack([real_part, imag_part], 1)

    blocks = lax.map(one_block, jnp.arange(16, dtype=jnp.int32))
    return jnp.transpose(blocks, (1, 2, 0, 3)).reshape(LOADS, 2, P_SIZE)


def panel_response(drive, mobility):
    highest = lax.Precision.HIGHEST
    drive_f = drive.astype(jnp.float32)
    mob_f = mobility.astype(jnp.float32)
    drive_re = drive_f[..., :K]
    drive_im = drive_f[..., K:]
    mob_re = mob_f[:, :, :K]
    mob_im = mob_f[:, :, K:]
    out_re = jnp.einsum("lsk,sjk->lsj", drive_re, mob_re, precision=highest) - jnp.einsum("lsk,sjk->lsj", drive_im, mob_im, precision=highest)
    out_im = jnp.einsum("lsk,sjk->lsj", drive_re, mob_im, precision=highest) + jnp.einsum("lsk,sjk->lsj", drive_im, mob_re, precision=highest)
    return jnp.concatenate([out_re, out_im], -1).astype(jnp.bfloat16)


def reference(impedance, mobility, force, patch_map, ownership):
    slot_patches = patch_map.reshape(P_SIZE // K, K)[ownership].reshape(P_SIZE).astype(jnp.int32)

    def to_natural(velocity_slots):
        values = velocity_slots.reshape(LOADS, P_SIZE // K, 2, K).transpose(0, 2, 1, 3).reshape(LOADS, 2, P_SIZE)
        return jnp.zeros((LOADS, 2, P_SIZE), jnp.bfloat16).at[:, :, slot_patches].set(values)

    def from_natural(field):
        return field[:, :, slot_patches].reshape(LOADS, 2, P_SIZE // K, K).transpose(0, 2, 1, 3).reshape(LOADS, P_SIZE // K, 2 * K)

    velocity = panel_response(force, mobility)
    pressure = jnp.zeros((LOADS, 2, P_SIZE), jnp.bfloat16)
    for iteration in range(ITERS):
        pressure = impedance_product(impedance, to_natural(velocity)).astype(jnp.bfloat16)
        drive = (force.astype(jnp.float32) - from_natural(pressure).astype(jnp.float32)).astype(jnp.bfloat16)
        velocity = panel_response(drive, mobility)
    return velocity, pressure
```

```python
import functools

import jax
import jax.numpy as jnp
from jax import lax
from jax.experimental import pallas as pl
from jax.experimental.pallas import tpu as pltpu
from jax.sharding import PartitionSpec as P

ITERS = 2
LANES = 128
BF16 = jnp.bfloat16
F32 = jnp.float32


MESH = pl.DeviceIdType.MESH


def gather_over_tile(tiles, x_ref, buf, send_sem, recv_sem, own_sem, ready):
    a_size = tiles // 4
    rows = x_ref.shape[0]
    half = rows // 2
    me = lax.axis_index("tile")
    core = lax.rem(me, 2)
    my_b = lax.rem(me // 2, 2)
    my_a = me // 4
    others = range(1, a_size)

    def chip_at(oa, ob):
        return lax.rem(my_a + oa, a_size) * 2 + lax.rem(my_b + ob, 2)

    def device_at(oa, ob):
        return chip_at(oa, ob) * 2 + core

    partner = chip_at(0, 0) * 2 + 1 - core
    neighbours = [partner, device_at(0, 1)] + [device_at(o, 0) for o in others]

    barrier = pltpu.get_barrier_semaphore()
    for device in neighbours:
        pl.semaphore_signal(barrier, inc=1, device_id={"tile": device}, device_id_type=MESH)
    pl.semaphore_wait(barrier, len(neighbours))

    def piece(oa, ob, h, owner_core):
        return buf.at[chip_at(oa, ob), pl.ds(pl.multiple_of(owner_core * rows + h * half, half), half)]

    sent = []

    def send(src, dst, device, relayed, oa, ob, h):
        copy = pltpu.make_async_remote_copy(
            src_ref=src,
            dst_ref=dst,
            send_sem=send_sem.at[len(sent)],
            recv_sem=recv_sem.at[relayed, oa * 2 + ob, h],
            device_id={"tile": device},
            device_id_type=MESH,
        )
        copy.start()
        sent.append(copy)

    def arrived(relayed, oa, ob, h):
        slot = piece(oa, ob, h, 1 - core if relayed else core)
        pltpu.make_async_remote_copy(
            src_ref=slot,
            dst_ref=slot,
            send_sem=send_sem.at[0],
            recv_sem=recv_sem.at[relayed, oa * 2 + ob, h],
            device_id={"tile": partner},
            device_id_type=MESH,
        ).wait_recv()

    def relay(oa, ob, h):
        slot = piece(oa, ob, h, core)
        send(slot, slot, partner, 1, oa, ob, h)

    def forward(oa, ob, h, device, new_oa, new_ob):
        slot = piece(oa, ob, h, core)
        send(slot, slot, device, 0, new_oa, new_ob, h)

    def own(h):
        return x_ref.at[pl.ds(h * half, half)]

    for h in (1, 0):
        send(own(h), piece(0, 0, h, core), device_at(0, 1), 0, 0, 1, h)
    for h in (0, 1):
        for o in others:
            send(own(h), piece(0, 0, h, core), device_at(o, 0), 0, (a_size - o) % a_size, 0, h)
    for h in (0, 1):
        send(own(h), piece(0, 0, h, core), partner, 1, 0, 0, h)
    local = pltpu.make_async_copy(
        x_ref, buf.at[chip_at(0, 0), pl.ds(pl.multiple_of(core * rows, rows), rows)], own_sem.at[0]
    )
    local.start()
    local.wait()
    for h in (0, 1):
        arrived(1, 0, 0, h)
    ready(chip_at(0, 0))

    arrived(0, 0, 1, 1)
    for o in others:
        forward(0, 1, 1, device_at(o, 0), (a_size - o) % a_size, 1)
    for o in others:
        arrived(0, o, 0, 0)
        forward(o, 0, 0, device_at(0, 1), o, 1)
    relay(0, 1, 1)
    for o in others:
        relay(o, 0, 0)
    arrived(0, 0, 1, 0)
    relay(0, 1, 0)
    for o in others:
        arrived(0, o, 0, 1)
        relay(o, 0, 1)
    for h in (1, 0):
        arrived(1, 0, 1, h)
    ready(chip_at(0, 1))
    for o in others:
        for h in (0, 1):
            arrived(0, o, 1, h)
            relay(o, 1, h)
    for o in others:
        for h in (0, 1):
            arrived(1, o, 0, h)
        ready(chip_at(o, 0))
    for o in others:
        for h in (0, 1):
            arrived(1, o, 1, h)
        ready(chip_at(o, 1))
    for copy in sent:
        copy.wait_send()


def gather_scratch(tiles, shape):
    a_size = tiles // 4
    copies = 2 + 2 * (a_size - 1) + 2 * (a_size - 1) + 2 * 2 * a_size
    return [
        pltpu.VMEM((tiles // 2, 2 * shape[0]) + shape[1:], BF16),
        pltpu.SemaphoreType.DMA((copies,)),
        pltpu.SemaphoreType.DMA((2, 2 * a_size, 2)),
        pltpu.SemaphoreType.DMA((1,)),
    ]


def pick_kernel(tiles, index_ref, x_ref, out_ref, buf, send_sem, recv_sem, own_sem):
    gather_over_tile(tiles, x_ref, buf, send_sem, recv_sem, own_sem, lambda chip: None)
    count = out_ref.shape[0]
    pair = buf.shape[1]
    step = 16

    @pl.loop(0, count // step)
    def _(block):
        base = block * step
        for k in range(step):
            index = index_ref[base + k]
            out_ref[base + k] = buf[index // pair, lax.rem(index, pair)]


def gather_and_pick(index, rows, tiles):
    return pl.pallas_call(
        functools.partial(pick_kernel, tiles),
        out_shape=jax.ShapeDtypeStruct((index.shape[0],) + rows.shape[1:], rows.dtype),
        in_specs=[
            pl.BlockSpec(memory_space=pltpu.SMEM),
            pl.BlockSpec(memory_space=pltpu.VMEM),
        ],
        out_specs=pl.BlockSpec(memory_space=pltpu.VMEM),
        scratch_shapes=gather_scratch(tiles, rows.shape),
        compiler_params=pltpu.CompilerParams(
            collective_id=0, has_side_effects=True, vmem_limit_bytes=40 * 2**20
        ),
    )(index, rows)


def couple_kernel(
    tiles,
    cols,
    block,
    z_ref,
    x_ref,
    out_ref,
    z_buf,
    z_sem,
    buf,
    part,
    sums,
    swap_send,
    swap_recv,
    own_sem,
    send_sem,
    recv_sem,
    sum_send,
    sum_recv,
):
    a_size = tiles // 4
    rows, width = out_ref.shape
    share = x_ref.shape[1]
    half = share // 2
    lanes = width // 2
    blocks = rows // block
    col = lax.axis_index("col")
    me = lax.axis_index("tile")
    core = lax.rem(me, 2)
    my_b = lax.rem(me // 2, 2)
    my_a = me // 4
    others = range(1, a_size)

    def chip_at(oa, ob):
        return lax.rem(my_a + oa, a_size) * 2 + lax.rem(my_b + ob, 2)

    def device_at(oa, ob):
        return chip_at(oa, ob) * 2 + core

    partner = chip_at(0, 0) * 2 + 1 - core
    neighbours = [partner, device_at(0, 1)] + [device_at(o, 0) for o in others]

    barrier = pltpu.get_barrier_semaphore()
    for device in neighbours:
        pl.semaphore_signal(barrier, inc=1, device_id={"tile": device}, device_id_type=MESH)
    for o in range(1, cols):
        pl.semaphore_signal(barrier, inc=1, device_id={"col": lax.rem(col + o, cols)}, device_id_type=MESH)

    def at(i):
        return pl.ds(pl.multiple_of(i * block, block), block)

    def fetch(i):
        return pltpu.make_async_copy(z_ref.at[:, at(i)], z_buf.at[:, at(i)], z_sem.at[i])

    @pl.loop(0, blocks)
    def _(i):
        fetch(i).start()

    near = jnp.minimum(col, cols - 1 - col)

    def group(k):
        side = col + (k + 1) // 2 if k % 2 else col - k // 2
        rest = jnp.where(near == col, k, cols - 1 - k)
        return jnp.where(k <= 2 * near, side, rest)

    order = [col] + [group(k) for k in range(1, cols)]

    def piece(g, oa, ob, h, owner_core):
        start = (chip_at(oa, ob) * 2 + owner_core) * share + h * half
        return buf.at[g, pl.ds(pl.multiple_of(start, half), half)]

    own_rows = pl.ds(pl.multiple_of(me * share, share), share)

    pl.semaphore_wait(barrier, len(neighbours) + cols - 1)

    def swap(k):
        return pltpu.make_async_remote_copy(
            src_ref=x_ref.at[order[k]],
            dst_ref=buf.at[col, own_rows],
            send_sem=swap_send.at[k - 1],
            recv_sem=swap_recv.at[col],
            device_id={"col": order[k]},
            device_id_type=MESH,
        )

    for k in range(1, cols):
        swap(k).start()

    sent = []

    def gather(k):
        g = order[k]

        def send(src, dst, device, relayed, oa, ob, h):
            copy = pltpu.make_async_remote_copy(
                src_ref=src,
                dst_ref=dst,
                send_sem=send_sem.at[len(sent)],
                recv_sem=recv_sem.at[k, relayed, oa * 2 + ob, h],
                device_id={"tile": device},
                device_id_type=MESH,
            )
            copy.start()
            sent.append(copy)

        def arrived(relayed, oa, ob, h):
            slot = piece(g, oa, ob, h, 1 - core if relayed else core)
            pltpu.make_async_remote_copy(
                src_ref=slot,
                dst_ref=slot,
                send_sem=send_sem.at[0],
                recv_sem=recv_sem.at[k, relayed, oa * 2 + ob, h],
                device_id={"tile": partner},
                device_id_type=MESH,
            ).wait_recv()

        def relay(oa, ob, h):
            slot = piece(g, oa, ob, h, core)
            send(slot, slot, partner, 1, oa, ob, h)

        def forward(oa, ob, h, device, new_oa, new_ob):
            slot = piece(g, oa, ob, h, core)
            send(slot, slot, device, 0, new_oa, new_ob, h)

        if k == 0:
            local = pltpu.make_async_copy(x_ref.at[g], buf.at[g, own_rows], own_sem.at[0])
            local.start()
            local.wait()
        else:
            slot = buf.at[g, own_rows]
            pltpu.make_async_remote_copy(
                src_ref=slot,
                dst_ref=slot,
                send_sem=swap_send.at[0],
                recv_sem=swap_recv.at[g],
                device_id={"col": g},
                device_id_type=MESH,
            ).wait_recv()
        for h in (1, 0):
            forward(0, 0, h, device_at(0, 1), 0, 1)
        for h in (0, 1):
            for o in others:
                forward(0, 0, h, device_at(o, 0), (a_size - o) % a_size, 0)
        for h in (0, 1):
            relay(0, 0, h)
        yield
        arrived(0, 0, 1, 1)
        for o in others:
            forward(0, 1, 1, device_at(o, 0), (a_size - o) % a_size, 1)
        for o in others:
            arrived(0, o, 0, 0)
            forward(o, 0, 0, device_at(0, 1), o, 1)
        relay(0, 1, 1)
        for o in others:
            relay(o, 0, 0)
        yield
        arrived(0, 0, 1, 0)
        relay(0, 1, 0)
        for o in others:
            arrived(0, o, 0, 1)
            relay(o, 0, 1)
        for h in (0, 1):
            for o in others:
                arrived(0, o, 1, h)
                relay(o, 1, h)
        for h in (0, 1):
            arrived(1, 0, 0, h)
        for h in (1, 0):
            arrived(1, 0, 1, h)
        for o in others:
            for h in (0, 1):
                arrived(1, o, 0, h)
        for o in others:
            for h in (0, 1):
                arrived(1, o, 1, h)
        yield

    last = cols - 1
    edge = jnp.logical_or(col == 0, col == last)

    def pass_on(g, i):
        below = jnp.logical_and(g < col, g == col - 1)
        slot = jnp.where(below, cols, g)
        return pltpu.make_async_remote_copy(
            src_ref=sums.at[g, at(i)],
            dst_ref=sums.at[slot, at(i)],
            send_sem=sum_send.at[g, i],
            recv_sem=sum_recv.at[slot, i],
            device_id={"col": jnp.where(g > col, col + 1, col - 1)},
            device_id_type=MESH,
        )

    def passed(slot, i):
        pltpu.make_async_remote_copy(
            src_ref=sums.at[slot, at(i)],
            dst_ref=sums.at[slot, at(i)],
            send_sem=sum_send.at[0, 0],
            recv_sem=sum_recv.at[slot, i],
            device_id={"col": lax.rem(col + 1, cols)},
            device_id_type=MESH,
        ).wait_recv()

    def multiply(k, low, high):
        g = order[k]

        @pl.loop(low, high)
        def _(i):
            if k == 0:
                fetch(i).wait()
            x = buf[g]
            a = jnp.dot(z_buf[0, at(i), :], x, preferred_element_type=F32)
            b = jnp.dot(z_buf[1, at(i), :], x, preferred_element_type=F32)
            term = jnp.concatenate([a[:, :lanes] - b[:, lanes:], a[:, lanes:] + b[:, :lanes]], 1)
            if k == 0:
                part[g, at(i), :] = term
            else:

                @pl.when(edge)
                def _():
                    sums[g, at(i), :] = term.astype(BF16)
                    pass_on(g, i).start()

                @pl.when(jnp.logical_not(edge))
                def _():
                    part[g, at(i), :] = term

    stages = [gather(k) for k in range(cols)]
    middle = blocks // 2
    next(stages[0])
    next(stages[0])
    if cols > 1:
        next(stages[1])
    next(stages[0])
    for k in range(cols):
        multiply(k, 0, middle)
        if k + 1 < cols:
            next(stages[k + 1])
        if k + 2 < cols:
            next(stages[k + 2])
        multiply(k, middle, blocks)
        if k + 1 < cols:
            next(stages[k + 1])

    lag = min(2, blocks)
    rising = 2 * col < cols

    def flow(up, turn, i):
        g = jnp.where(up, turn, last - turn)
        due = jnp.where(up, g - col, col - g) > 0

        @pl.when(due)
        def _():
            passed(g, i)
            sums[g, at(i), :] = (sums[g, at(i), :].astype(F32) + part[g, at(i), :]).astype(BF16)
            pass_on(g, i).start()

    @pl.when(jnp.logical_not(edge))
    def _():
        for turn in range(1, cols):

            @pl.loop(0, blocks + lag)
            def _(i):
                @pl.when(i < blocks)
                def _():
                    flow(rising, turn, i)

                @pl.when(i >= lag)
                def _():
                    flow(jnp.logical_not(rising), turn, i - lag)

    @pl.loop(0, blocks)
    def _(i):
        @pl.when(col > 0)
        def _():
            passed(col, i)
            part[col, at(i), :] += sums[col, at(i), :].astype(F32)

        @pl.when(col < last)
        def _():
            passed(cols, i)
            part[col, at(i), :] += sums[cols, at(i), :].astype(F32)

        out_ref[at(i), :] = part[col, at(i), :].astype(BF16)

    for k in range(1, cols):

        @pl.loop(0, blocks)
        def _(i):
            pass_on(order[k], i).wait_send()

    for k in range(1, cols):
        swap(k).wait_send()
    for copy in sent:
        copy.wait_send()


def couple(impedance, x, tiles):
    _, rows, depth = impedance.shape
    cols, share, width = x.shape
    a_size = tiles // 4
    block = min(256, rows)
    copies = cols * (2 + 2 * (a_size - 1) + 2 * (a_size - 1) + 2 * 2 * a_size)
    return pl.pallas_call(
        functools.partial(couple_kernel, tiles, cols, block),
        out_shape=jax.ShapeDtypeStruct((rows, width), BF16),
        in_specs=[
            pl.BlockSpec(memory_space=pl.ANY),
            pl.BlockSpec(memory_space=pltpu.VMEM),
        ],
        out_specs=pl.BlockSpec(memory_space=pltpu.VMEM),
        scratch_shapes=[
            pltpu.VMEM((2, rows, depth), BF16),
            pltpu.SemaphoreType.DMA((rows // block,)),
            pltpu.VMEM((cols, depth, width), BF16),
            pltpu.VMEM((cols, rows, width), F32),
            pltpu.VMEM((cols + 1, rows, width), BF16),
            pltpu.SemaphoreType.DMA((max(cols - 1, 1),)),
            pltpu.SemaphoreType.DMA((cols,)),
            pltpu.SemaphoreType.DMA((1,)),
            pltpu.SemaphoreType.DMA((copies,)),
            pltpu.SemaphoreType.DMA((cols, 2, 2 * a_size, 2)),
            pltpu.SemaphoreType.DMA((cols, rows // block)),
            pltpu.SemaphoreType.DMA((cols + 1, rows // block)),
        ],
        compiler_params=pltpu.CompilerParams(
            collective_id=1, has_side_effects=True, vmem_limit_bytes=60 * 2**20
        ),
    )(impedance, x)


def inverse_permutation(sigma):
    count = sigma.shape[0]
    where = jnp.arange(count, dtype=jnp.int32)
    high = (sigma // LANES)[None, :] == jnp.arange(count // LANES, dtype=jnp.int32)[:, None]
    low = (sigma % LANES)[:, None] == jnp.arange(LANES, dtype=jnp.int32)[None, :]
    where_high = jnp.where(low, (where // LANES)[:, None], 0).astype(BF16)
    where_low = jnp.where(low, (where % LANES)[:, None], 0).astype(BF16)
    digits = jnp.dot(
        high.astype(BF16), jnp.concatenate([where_high, where_low], 1), preferred_element_type=F32
    )
    inverse = digits[:, :LANES] * LANES + digits[:, LANES:]
    return inverse.astype(jnp.int32).reshape(count)


def per_device(impedance, mobility, force, patch_map, ownership):
    slots, width, _ = mobility.shape
    patches = patch_map.shape[0]
    loads = force.shape[0]
    tiles = lax.axis_size("tile")
    cols = lax.axis_size("col")
    share = patches // cols // tiles
    mine = slots * width
    tile = lax.axis_index("tile")

    panels = patch_map.reshape(-1, width)
    slot_flat = panels[ownership].reshape(mine)
    owners = lax.all_gather(ownership, "tile", axis=0, tiled=True)
    inverse = inverse_permutation(panels[owners].reshape(patches))
    share_index = lax.dynamic_index_in_dim(
        inverse.reshape(cols, tiles, share), tile, 1, keepdims=False
    ).reshape(cols * share)

    mob_re = mobility[:, :, :width]
    mob_im = mobility[:, :, width:]
    form = jnp.stack(
        [jnp.stack([mob_re, -mob_im], -1), jnp.stack([mob_im, mob_re], -1)], 2
    ).reshape(slots, 2 * width, 2 * width)
    force_rows = force.reshape(loads, slots, 2, width).transpose(1, 3, 2, 0).reshape(slots, 2 * width, loads)

    def response(drive):
        return lax.dot_general(
            form, drive, (((2,), (1,)), ((0,), (0,))), preferred_element_type=F32
        ).astype(BF16)

    velocity = response(force_rows)
    for _ in range(ITERS):
        picked = gather_and_pick(share_index, velocity.reshape(mine, 2, loads), tiles)
        summed = couple(impedance, picked.reshape(cols, share, 2 * loads), tiles)
        pressure = summed.reshape(-1, 2, loads)
        at_slots = gather_and_pick(slot_flat, pressure, tiles).reshape(slots, 2 * width, loads)
        drive = (force_rows.astype(F32) - at_slots.astype(F32)).astype(BF16)
        velocity = response(drive)
    velocity_out = velocity.reshape(slots, width, 2, loads).transpose(3, 0, 2, 1).reshape(loads, slots, 2 * width)
    pressure_out = pressure.transpose(2, 1, 0)
    return velocity_out, pressure_out


def solution(mesh):
    return jax.shard_map(
        per_device,
        mesh=mesh,
        in_specs=(
            P(None, "tile", "col"),
            P("tile", None, None),
            P("col", "tile", None),
            P(),
            P("tile"),
        ),
        out_specs=(P("col", "tile", None), P("col", None, "tile")),
        check_vma=False,
    )
```

```python
import functools

import jax
import jax.numpy as jnp
from jax import lax
from jax.experimental import pallas as pl
from jax.experimental.pallas import tpu as pltpu
from jax.sharding import PartitionSpec as P

ITERS = 2
LANES = 128
BF16 = jnp.bfloat16
F32 = jnp.float32


MESH = pl.DeviceIdType.MESH


def gather_over_tile(tiles, x_ref, buf, send_sem, recv_sem, own_sem):
    a_size = tiles // 4
    rows = x_ref.shape[0]
    half = rows // 2
    me = lax.axis_index("tile")
    core = lax.rem(me, 2)
    my_b = lax.rem(me // 2, 2)
    my_a = me // 4
    others = range(1, a_size)

    def chip_at(oa, ob):
        return lax.rem(my_a + oa, a_size) * 2 + lax.rem(my_b + ob, 2)

    def device_at(oa, ob):
        return chip_at(oa, ob) * 2 + core

    partner = chip_at(0, 0) * 2 + 1 - core
    neighbours = [partner, device_at(0, 1)] + [device_at(o, 0) for o in others]

    barrier = pltpu.get_barrier_semaphore()
    for device in neighbours:
        pl.semaphore_signal(barrier, inc=1, device_id={"tile": device}, device_id_type=MESH)
    pl.semaphore_wait(barrier, len(neighbours))

    def piece(oa, ob, h, owner_core):
        start = (chip_at(oa, ob) * 2 + owner_core) * rows + h * half
        return buf.at[pl.ds(pl.multiple_of(start, half), half)]

    sent = []

    def send(src, dst, device, relayed, oa, ob, h):
        copy = pltpu.make_async_remote_copy(
            src_ref=src,
            dst_ref=dst,
            send_sem=send_sem.at[len(sent)],
            recv_sem=recv_sem.at[relayed, oa * 2 + ob, h],
            device_id={"tile": device},
            device_id_type=MESH,
        )
        copy.start()
        sent.append(copy)

    def arrived(relayed, oa, ob, h):
        slot = piece(oa, ob, h, 1 - core if relayed else core)
        pltpu.make_async_remote_copy(
            src_ref=slot,
            dst_ref=slot,
            send_sem=send_sem.at[0],
            recv_sem=recv_sem.at[relayed, oa * 2 + ob, h],
            device_id={"tile": partner},
            device_id_type=MESH,
        ).wait_recv()

    def relay(oa, ob, h):
        slot = piece(oa, ob, h, core)
        send(slot, slot, partner, 1, oa, ob, h)

    def forward(oa, ob, h, device, new_oa, new_ob):
        slot = piece(oa, ob, h, core)
        send(slot, slot, device, 0, new_oa, new_ob, h)

    def own(h):
        return x_ref.at[pl.ds(h * half, half)]

    for h in (1, 0):
        send(own(h), piece(0, 0, h, core), device_at(0, 1), 0, 0, 1, h)
    for h in (0, 1):
        for o in others:
            send(own(h), piece(0, 0, h, core), device_at(o, 0), 0, (a_size - o) % a_size, 0, h)
    for h in (0, 1):
        send(own(h), piece(0, 0, h, core), partner, 1, 0, 0, h)
    local = pltpu.make_async_copy(
        x_ref, buf.at[pl.ds(pl.multiple_of(me * rows, rows), rows)], own_sem.at[0]
    )
    local.start()
    local.wait()
    for h in (0, 1):
        arrived(1, 0, 0, h)

    arrived(0, 0, 1, 1)
    for o in others:
        forward(0, 1, 1, device_at(o, 0), (a_size - o) % a_size, 1)
    for o in others:
        arrived(0, o, 0, 0)
        forward(o, 0, 0, device_at(0, 1), o, 1)
    relay(0, 1, 1)
    for o in others:
        relay(o, 0, 0)
    arrived(0, 0, 1, 0)
    relay(0, 1, 0)
    for o in others:
        arrived(0, o, 0, 1)
        relay(o, 0, 1)
    for h in (1, 0):
        arrived(1, 0, 1, h)
    for o in others:
        for h in (0, 1):
            arrived(0, o, 1, h)
            relay(o, 1, h)
    for o in others:
        for h in (0, 1):
            arrived(1, o, 0, h)
    for o in others:
        for h in (0, 1):
            arrived(1, o, 1, h)
    for copy in sent:
        copy.wait_send()


def gather_scratch(tiles, shape):
    a_size = tiles // 4
    copies = 2 + 2 * (a_size - 1) + 2 * (a_size - 1) + 2 * 2 * a_size
    return [
        pltpu.VMEM((tiles * shape[0],) + shape[1:], BF16),
        pltpu.SemaphoreType.DMA((copies,)),
        pltpu.SemaphoreType.DMA((2, 2 * a_size, 2)),
        pltpu.SemaphoreType.DMA((1,)),
    ]


def pick_kernel(tiles, index_ref, x_ref, out_ref, buf, send_sem, recv_sem, own_sem):
    gather_over_tile(tiles, x_ref, buf, send_sem, recv_sem, own_sem)
    count = out_ref.shape[0]
    step = 32

    @pl.loop(0, count // step)
    def _(block):
        base = block * step
        for k in range(step):
            out_ref[base + k] = buf[index_ref[base + k]]


def gather_and_pick(index, rows, tiles):
    return pl.pallas_call(
        functools.partial(pick_kernel, tiles),
        out_shape=jax.ShapeDtypeStruct((index.shape[0],) + rows.shape[1:], rows.dtype),
        in_specs=[
            pl.BlockSpec(memory_space=pltpu.SMEM),
            pl.BlockSpec(memory_space=pltpu.VMEM),
        ],
        out_specs=pl.BlockSpec(memory_space=pltpu.VMEM),
        scratch_shapes=gather_scratch(tiles, rows.shape),
        compiler_params=pltpu.CompilerParams(
            collective_id=0, has_side_effects=True, vmem_limit_bytes=40 * 2**20
        ),
    )(index, rows)


def couple_kernel(
    tiles,
    cols,
    block,
    z_ref,
    x_ref,
    out_ref,
    z_buf,
    z_sem,
    buf,
    part,
    sums,
    swap_send,
    swap_recv,
    own_sem,
    send_sem,
    recv_sem,
    sum_send,
    sum_recv,
):
    a_size = tiles // 4
    rows, width = out_ref.shape
    share = x_ref.shape[1]
    half = share // 2
    lanes = width // 2
    blocks = rows // block
    height = min(2 * block, rows)
    each = height // block
    steps = rows // height
    col = lax.axis_index("col")
    me = lax.axis_index("tile")
    core = lax.rem(me, 2)
    my_b = lax.rem(me // 2, 2)
    my_a = me // 4
    others = range(1, a_size)

    def chip_at(oa, ob):
        return lax.rem(my_a + oa, a_size) * 2 + lax.rem(my_b + ob, 2)

    def device_at(oa, ob):
        return chip_at(oa, ob) * 2 + core

    partner = chip_at(0, 0) * 2 + 1 - core
    neighbours = [partner, device_at(0, 1)] + [device_at(o, 0) for o in others]

    barrier = pltpu.get_barrier_semaphore()
    for device in neighbours:
        pl.semaphore_signal(barrier, inc=1, device_id={"tile": device}, device_id_type=MESH)
    for o in range(1, cols):
        pl.semaphore_signal(barrier, inc=1, device_id={"col": lax.rem(col + o, cols)}, device_id_type=MESH)

    def at(i):
        return pl.ds(pl.multiple_of(i * block, block), block)

    def tall(t):
        return pl.ds(pl.multiple_of(t * height, height), height)

    def fetch(t):
        return pltpu.make_async_copy(z_ref.at[:, tall(t)], z_buf.at[:, tall(t)], z_sem.at[t])

    @pl.loop(0, steps)
    def _(i):
        fetch(i).start()

    last = cols - 1
    edge = jnp.logical_or(col == 0, col == last)
    near = jnp.minimum(col, last - col)

    def group(k):
        side = col + (k + 1) // 2 if k % 2 else col - k // 2
        rest = jnp.where(near == col, k, last - k)
        return jnp.where(k <= 2 * near, side, rest)

    others_col = [group(k) for k in range(1, cols)]
    order = [jnp.where(edge, a, b) for a, b in zip(others_col + [col], [col] + others_col)]

    def piece(g, oa, ob, h, owner_core):
        start = (chip_at(oa, ob) * 2 + owner_core) * share + h * half
        return buf.at[g, pl.ds(pl.multiple_of(start, half), half)]

    own_rows = pl.ds(pl.multiple_of(me * share, share), share)

    pl.semaphore_wait(barrier, len(neighbours) + cols - 1)

    def swap(k):
        return pltpu.make_async_remote_copy(
            src_ref=x_ref.at[others_col[k]],
            dst_ref=buf.at[col, own_rows],
            send_sem=swap_send.at[k],
            recv_sem=swap_recv.at[col],
            device_id={"col": others_col[k]},
            device_id_type=MESH,
        )

    for k in range(last):
        swap(k).start()
    own = pltpu.make_async_copy(x_ref.at[col], buf.at[col, own_rows], own_sem.at[0])
    own.start()
    own.wait()

    sends = [0]

    def gather(k):
        g = order[k]

        def send(src, dst, device, relayed, oa, ob, h):
            copy = pltpu.make_async_remote_copy(
                src_ref=src,
                dst_ref=dst,
                send_sem=send_sem.at[sends[0]],
                recv_sem=recv_sem.at[k, relayed, oa * 2 + ob, h],
                device_id={"tile": device},
                device_id_type=MESH,
            )
            copy.start()
            sends[0] += 1

        def arrived(relayed, oa, ob, h):
            slot = piece(g, oa, ob, h, 1 - core if relayed else core)
            pltpu.make_async_remote_copy(
                src_ref=slot,
                dst_ref=slot,
                send_sem=send_sem.at[0],
                recv_sem=recv_sem.at[k, relayed, oa * 2 + ob, h],
                device_id={"tile": partner},
                device_id_type=MESH,
            ).wait_recv()

        def relay(oa, ob, h):
            slot = piece(g, oa, ob, h, core)
            send(slot, slot, partner, 1, oa, ob, h)

        def forward(oa, ob, h, device, new_oa, new_ob):
            slot = piece(g, oa, ob, h, core)
            send(slot, slot, device, 0, new_oa, new_ob, h)

        @pl.when(g != col)
        def _():
            slot = buf.at[g, own_rows]
            pltpu.make_async_remote_copy(
                src_ref=slot,
                dst_ref=slot,
                send_sem=swap_send.at[0],
                recv_sem=swap_recv.at[g],
                device_id={"col": lax.rem(col + 1, cols)},
                device_id_type=MESH,
            ).wait_recv()

        for h in (1, 0):
            forward(0, 0, h, device_at(0, 1), 0, 1)
        for h in (0, 1):
            for o in others:
                forward(0, 0, h, device_at(o, 0), (a_size - o) % a_size, 0)
        for h in (0, 1):
            relay(0, 0, h)
        yield
        arrived(0, 0, 1, 1)
        for o in others:
            forward(0, 1, 1, device_at(o, 0), (a_size - o) % a_size, 1)
        for o in others:
            arrived(0, o, 0, 0)
            forward(o, 0, 0, device_at(0, 1), o, 1)
        relay(0, 1, 1)
        for o in others:
            relay(o, 0, 0)
        yield
        arrived(0, 0, 1, 0)
        relay(0, 1, 0)
        for o in others:
            arrived(0, o, 0, 1)
            relay(o, 0, 1)
        for h in (0, 1):
            for o in others:
                arrived(0, o, 1, h)
                relay(o, 1, h)
        for h in (0, 1):
            arrived(1, 0, 0, h)
        for h in (1, 0):
            arrived(1, 0, 1, h)
        for o in others:
            for h in (0, 1):
                arrived(1, o, 0, h)
        for o in others:
            for h in (0, 1):
                arrived(1, o, 1, h)
        yield

    def pass_on(g, i):
        below = jnp.logical_and(g < col, g == col - 1)
        slot = jnp.where(below, cols, g)
        return pltpu.make_async_remote_copy(
            src_ref=sums.at[g, at(i)],
            dst_ref=sums.at[slot, at(i)],
            send_sem=sum_send.at[g, i],
            recv_sem=sum_recv.at[slot, i],
            device_id={"col": jnp.where(g > col, col + 1, col - 1)},
            device_id_type=MESH,
        )

    def passed(slot, i):
        pltpu.make_async_remote_copy(
            src_ref=sums.at[slot, at(i)],
            dst_ref=sums.at[slot, at(i)],
            send_sem=sum_send.at[0, 0],
            recv_sem=sum_recv.at[slot, i],
            device_id={"col": lax.rem(col + 1, cols)},
            device_id_type=MESH,
        ).wait_recv()

    lag = min(2, blocks)
    rising = 2 * col < cols

    def flow(up, turn, i):
        g = jnp.where(up, turn, last - turn)
        due = jnp.where(up, g - col, col - g) > 0

        @pl.when(due)
        def _():
            passed(g, i)
            sums[g, at(i), :] = (sums[g, at(i), :].astype(F32) + part[g, at(i), :]).astype(BF16)
            pass_on(g, i).start()

    def multiply(k, midway):
        g = order[k]
        ends = jnp.logical_and(edge, g != col)

        @pl.loop(0, steps)
        def _(t):
            @pl.when(t == steps // 2)
            def _():
                midway()

            if k == 0:
                fetch(t).wait()
            at_t = tall(t)
            x = buf[g]
            a = jnp.dot(z_buf[0, at_t, :], x, preferred_element_type=F32)
            b = jnp.dot(z_buf[1, at_t, :], x, preferred_element_type=F32)
            term = jnp.concatenate([a[:, :lanes] - b[:, lanes:], a[:, lanes:] + b[:, :lanes]], 1)

            @pl.when(ends)
            def _():
                sums[g, at_t, :] = term.astype(BF16)
                for n in range(each):
                    pass_on(g, t * each + n).start()

            @pl.when(jnp.logical_not(ends))
            def _():
                part[g, at_t, :] = term

            if k == last and cols > 2:

                @pl.when(jnp.logical_not(edge))
                def _():
                    for n in range(each):
                        flow(rising, 2, t * each + n)
                        flow(jnp.logical_not(rising), 2, t * each + n)

    stages = [gather(k) for k in range(cols)]
    def advance(k):
        if k < cols:
            next(stages[k])

    advance(0)
    advance(0)
    advance(1)
    advance(0)
    for k in range(cols):

        def midway():
            advance(k + 1)
            advance(k + 2)

        multiply(k, midway)
        advance(k + 1)

    @pl.when(jnp.logical_not(edge))
    def _():
        for turn in range(3, cols):

            @pl.loop(0, blocks + lag)
            def _(i):
                @pl.when(i < blocks)
                def _():
                    flow(rising, turn, i)

                @pl.when(i >= lag)
                def _():
                    flow(jnp.logical_not(rising), turn, i - lag)

    @pl.loop(0, blocks)
    def _(i):
        @pl.when(col > 0)
        def _():
            passed(col, i)
            part[col, at(i), :] += sums[col, at(i), :].astype(F32)

        @pl.when(col < last)
        def _():
            passed(cols, i)
            part[col, at(i), :] += sums[cols, at(i), :].astype(F32)

        out_ref[at(i), :] = part[col, at(i), :].astype(BF16)

    for g in others_col:

        @pl.loop(0, blocks)
        def _(i):
            pass_on(g, i).wait_send()

    for k in range(last):
        swap(k).wait_send()
    for n in range(sends[0]):
        slot = piece(0, 0, 0, 0, core)
        pltpu.make_async_remote_copy(
            src_ref=slot,
            dst_ref=slot,
            send_sem=send_sem.at[n],
            recv_sem=recv_sem.at[0, 0, 0, 0],
            device_id={"tile": partner},
            device_id_type=MESH,
        ).wait_send()


def couple(impedance, x, tiles):
    _, rows, depth = impedance.shape
    cols, share, width = x.shape
    a_size = tiles // 4
    block = min(256, rows)
    copies = cols * (2 + 2 * (a_size - 1) + 2 * (a_size - 1) + 2 * 2 * a_size)
    return pl.pallas_call(
        functools.partial(couple_kernel, tiles, cols, block),
        out_shape=jax.ShapeDtypeStruct((rows, width), BF16),
        in_specs=[
            pl.BlockSpec(memory_space=pl.ANY),
            pl.BlockSpec(memory_space=pltpu.VMEM),
        ],
        out_specs=pl.BlockSpec(memory_space=pltpu.VMEM),
        scratch_shapes=[
            pltpu.VMEM((2, rows, depth), BF16),
            pltpu.SemaphoreType.DMA((rows // block,)),
            pltpu.VMEM((cols, depth, width), BF16),
            pltpu.VMEM((cols, rows, width), F32),
            pltpu.VMEM((cols + 1, rows, width), BF16),
            pltpu.SemaphoreType.DMA((max(cols - 1, 1),)),
            pltpu.SemaphoreType.DMA((cols,)),
            pltpu.SemaphoreType.DMA((1,)),
            pltpu.SemaphoreType.DMA((copies,)),
            pltpu.SemaphoreType.DMA((cols, 2, 2 * a_size, 2)),
            pltpu.SemaphoreType.DMA((cols, rows // block)),
            pltpu.SemaphoreType.DMA((cols + 1, rows // block)),
        ],
        compiler_params=pltpu.CompilerParams(
            collective_id=1, has_side_effects=True, vmem_limit_bytes=60 * 2**20
        ),
    )(impedance, x)


def places_of(sigma, tile, cols, tiles):
    count = sigma.shape[0]
    per = count // cols // tiles // LANES
    where = jnp.arange(count, dtype=jnp.int32)
    col = jnp.arange(cols, dtype=jnp.int32)[:, None]
    heads = ((col * tiles + tile) * per + jnp.arange(per, dtype=jnp.int32)[None, :]).reshape(-1)
    high = (sigma // LANES)[None, :] == heads[:, None]
    low = (sigma % LANES)[None, :] == jnp.arange(LANES, dtype=jnp.int32)[:, None]
    digits = jnp.stack([where // LANES, where % LANES])
    left = jnp.where(high[None], digits[:, None, :], 0).astype(BF16).reshape(-1, count)
    found = lax.dot_general(
        left, low.astype(BF16), (((1,), (1,)), ((), ())), preferred_element_type=F32
    ).reshape(2, -1)
    return (found[0] * LANES + found[1]).astype(jnp.int32)


def per_device(impedance, mobility, force, patch_map, ownership):
    slots, width, _ = mobility.shape
    patches = patch_map.shape[0]
    loads = force.shape[0]
    tiles = lax.axis_size("tile")
    cols = lax.axis_size("col")
    share = patches // cols // tiles
    mine = slots * width
    tile = lax.axis_index("tile")

    panels = patch_map.reshape(-1, width)
    slot_flat = panels[ownership].reshape(mine)
    owners = lax.all_gather(ownership, "tile", axis=0, tiled=True)
    share_index = places_of(panels[owners].reshape(patches), tile, cols, tiles)

    mob_re = mobility[:, :, :width]
    mob_im = mobility[:, :, width:]
    plain = jnp.concatenate(
        [jnp.concatenate([mob_re, -mob_im], 2), jnp.concatenate([mob_im, mob_re], 2)], 1
    )
    entry = jnp.arange(2 * width, dtype=jnp.int32)
    mixed = (entry % 2) * width + entry // 2
    mix = (mixed[:, None] == entry[None, :]).astype(BF16)

    def product(a, a_dim, b, b_dim, a_batch=0, b_batch=0):
        return lax.dot_general(a, b, (((a_dim,), (b_dim,)), ((a_batch,), (b_batch,))), preferred_element_type=F32)

    def rows_mixed(a):
        many = jnp.broadcast_to(mix, (slots,) + mix.shape)
        return product(many, 2, a, 1).astype(BF16)

    by_pair = lax.dot_general(plain, mix, (((2,), (1,)), ((), ())), preferred_element_type=F32).astype(BF16)
    pair_force = rows_mixed(plain)
    pair_pair = rows_mixed(by_pair)
    first = product(pair_force, 2, force, 2, 0, 1)
    first_out = product(force, 2, plain, 2, 1, 0)

    velocity = first.astype(BF16)
    for turn in range(ITERS):
        picked = gather_and_pick(share_index, velocity.reshape(mine, 2, loads), tiles)
        summed = couple(impedance, picked.reshape(cols, share, 2 * loads), tiles)
        pressure = summed.reshape(-1, 2, loads)
        at_slots = gather_and_pick(slot_flat, pressure, tiles).reshape(slots, 2 * width, loads)
        if turn < ITERS - 1:
            velocity = (first - product(pair_pair, 2, at_slots, 1)).astype(BF16)
    velocity_out = (first_out - product(at_slots, 1, by_pair, 2)).astype(BF16).transpose(1, 0, 2)
    pressure_out = pressure.transpose(2, 1, 0)
    return velocity_out, pressure_out


def solution(mesh):
    return jax.shard_map(
        per_device,
        mesh=mesh,
        in_specs=(
            P(None, "tile", "col"),
            P("tile", None, None),
            P("col", "tile", None),
            P(),
            P("tile"),
        ),
        out_specs=(P("col", "tile", None), P("col", None, "tile")),
        check_vma=False,
    )
```

```python
import functools

import jax
import jax.numpy as jnp
from jax import lax
from jax.experimental import pallas as pl
from jax.experimental.pallas import tpu as pltpu
from jax.sharding import PartitionSpec as P

ITERS = 2
LANES = 128
BF16 = jnp.bfloat16
F32 = jnp.float32


MESH = pl.DeviceIdType.MESH


def gather_over_tile(tiles, x_ref, buf, send_sem, recv_sem, own_sem):
    a_size = tiles // 4
    rows = x_ref.shape[0]
    half = rows // 2
    me = lax.axis_index("tile")
    core = lax.rem(me, 2)
    my_b = lax.rem(me // 2, 2)
    my_a = me // 4
    others = range(1, a_size)

    def chip_at(oa, ob):
        return lax.rem(my_a + oa, a_size) * 2 + lax.rem(my_b + ob, 2)

    def device_at(oa, ob):
        return chip_at(oa, ob) * 2 + core

    partner = chip_at(0, 0) * 2 + 1 - core
    neighbours = [partner, device_at(0, 1)] + [device_at(o, 0) for o in others]

    barrier = pltpu.get_barrier_semaphore()
    for device in neighbours:
        pl.semaphore_signal(barrier, inc=1, device_id={"tile": device}, device_id_type=MESH)
    pl.semaphore_wait(barrier, len(neighbours))

    def piece(oa, ob, h, owner_core):
        start = (chip_at(oa, ob) * 2 + owner_core) * rows + h * half
        return buf.at[pl.ds(pl.multiple_of(start, half), half)]

    sent = []

    def send(src, dst, device, relayed, oa, ob, h):
        copy = pltpu.make_async_remote_copy(
            src_ref=src,
            dst_ref=dst,
            send_sem=send_sem.at[len(sent)],
            recv_sem=recv_sem.at[relayed, oa * 2 + ob, h],
            device_id={"tile": device},
            device_id_type=MESH,
        )
        copy.start()
        sent.append(copy)

    def arrived(relayed, oa, ob, h):
        slot = piece(oa, ob, h, 1 - core if relayed else core)
        pltpu.make_async_remote_copy(
            src_ref=slot,
            dst_ref=slot,
            send_sem=send_sem.at[0],
            recv_sem=recv_sem.at[relayed, oa * 2 + ob, h],
            device_id={"tile": partner},
            device_id_type=MESH,
        ).wait_recv()

    def relay(oa, ob, h):
        slot = piece(oa, ob, h, core)
        send(slot, slot, partner, 1, oa, ob, h)

    def forward(oa, ob, h, device, new_oa, new_ob):
        slot = piece(oa, ob, h, core)
        send(slot, slot, device, 0, new_oa, new_ob, h)

    def own(h):
        return x_ref.at[pl.ds(h * half, half)]

    for h in (1, 0):
        send(own(h), piece(0, 0, h, core), device_at(0, 1), 0, 0, 1, h)
    for h in (0, 1):
        for o in others:
            send(own(h), piece(0, 0, h, core), device_at(o, 0), 0, (a_size - o) % a_size, 0, h)
    for h in (0, 1):
        send(own(h), piece(0, 0, h, core), partner, 1, 0, 0, h)
    local = pltpu.make_async_copy(
        x_ref, buf.at[pl.ds(pl.multiple_of(me * rows, rows), rows)], own_sem.at[0]
    )
    local.start()
    local.wait()
    for h in (0, 1):
        arrived(1, 0, 0, h)

    arrived(0, 0, 1, 1)
    for o in others:
        forward(0, 1, 1, device_at(o, 0), (a_size - o) % a_size, 1)
    for o in others:
        arrived(0, o, 0, 0)
        forward(o, 0, 0, device_at(0, 1), o, 1)
    relay(0, 1, 1)
    for o in others:
        relay(o, 0, 0)
    arrived(0, 0, 1, 0)
    relay(0, 1, 0)
    for o in others:
        arrived(0, o, 0, 1)
        relay(o, 0, 1)
    for h in (1, 0):
        arrived(1, 0, 1, h)
    for o in others:
        for h in (0, 1):
            arrived(0, o, 1, h)
            relay(o, 1, h)
    for o in others:
        for h in (0, 1):
            arrived(1, o, 0, h)
    for o in others:
        for h in (0, 1):
            arrived(1, o, 1, h)
    for copy in sent:
        copy.wait_send()


def gather_scratch(tiles, shape):
    a_size = tiles // 4
    copies = 2 + 2 * (a_size - 1) + 2 * (a_size - 1) + 2 * 2 * a_size
    return [
        pltpu.VMEM((tiles * shape[0],) + shape[1:], BF16),
        pltpu.SemaphoreType.DMA((copies,)),
        pltpu.SemaphoreType.DMA((2, 2 * a_size, 2)),
        pltpu.SemaphoreType.DMA((1,)),
    ]


def pick_kernel(tiles, index_ref, x_ref, out_ref, buf, send_sem, recv_sem, own_sem):
    gather_over_tile(tiles, x_ref, buf, send_sem, recv_sem, own_sem)
    count = out_ref.shape[0]
    step = 32

    @pl.loop(0, count // step)
    def _(block):
        base = block * step
        for k in range(step):
            out_ref[base + k] = buf[index_ref[base + k]]


def gather_and_pick(index, rows, tiles):
    return pl.pallas_call(
        functools.partial(pick_kernel, tiles),
        out_shape=jax.ShapeDtypeStruct((index.shape[0],) + rows.shape[1:], rows.dtype),
        in_specs=[
            pl.BlockSpec(memory_space=pltpu.SMEM),
            pl.BlockSpec(memory_space=pltpu.VMEM),
        ],
        out_specs=pl.BlockSpec(memory_space=pltpu.VMEM),
        scratch_shapes=gather_scratch(tiles, rows.shape),
        compiler_params=pltpu.CompilerParams(
            collective_id=0, has_side_effects=True, vmem_limit_bytes=40 * 2**20
        ),
    )(index, rows)


def couple_kernel(
    tiles,
    cols,
    index_ref,
    z_ref,
    x_ref,
    out_ref,
    own_ref,
    z_buf,
    z_sem,
    buf,
    part,
    sums,
    whole,
    swap_send,
    swap_recv,
    own_sem,
    send_sem,
    recv_sem,
    sum_send,
    sum_recv,
):
    a_size = tiles // 4
    rows, _, lanes = own_ref.shape
    share = x_ref.shape[1]
    height = rows // 4
    each = 4
    block = height // each
    blocks = rows // block
    slots = z_buf.shape[0]
    col = lax.axis_index("col")
    me = lax.axis_index("tile")
    core = lax.rem(me, 2)
    my_b = lax.rem(me // 2, 2)
    my_a = me // 4
    others = range(1, a_size)

    def chip_at(oa, ob):
        return lax.rem(my_a + oa, a_size) * 2 + lax.rem(my_b + ob, 2)

    def device_at(oa, ob):
        return chip_at(oa, ob) * 2 + core

    partner = chip_at(0, 0) * 2 + 1 - core
    neighbours = [partner, device_at(0, 1)] + [device_at(o, 0) for o in others]

    barrier = pltpu.get_barrier_semaphore()
    for device in neighbours:
        pl.semaphore_signal(barrier, inc=1, device_id={"tile": device}, device_id_type=MESH)
    for o in range(1, cols):
        pl.semaphore_signal(barrier, inc=1, device_id={"col": lax.rem(col + o, cols)}, device_id_type=MESH)

    def at(i):
        return pl.ds(pl.multiple_of(i * block, block), block)

    def tall(t):
        return pl.ds(pl.multiple_of(t * height, height), height)

    def fetch(t):
        slot = lax.rem(t, slots)
        return pltpu.make_async_copy(z_ref.at[:, tall(t)], z_buf.at[slot], z_sem.at[t])

    for t in range(3):
        fetch(t).start()

    last = cols - 1
    edge = jnp.logical_or(col == 0, col == last)
    inner = jnp.logical_not(edge)
    near = jnp.minimum(col, last - col)

    def group(k):
        side = col + (k + 1) // 2 if k % 2 else col - k // 2
        rest = jnp.where(near == col, k, last - k)
        return jnp.where(k <= 2 * near, side, rest)

    others_col = [group(k) for k in range(1, cols)]
    order = [jnp.where(edge, a, b) for a, b in zip(others_col + [col], [col] + others_col)]

    def order_at(k):
        g = order[0]
        for n in range(1, cols):
            g = jnp.where(k == n, order[n], g)
        return g

    own_rows = pl.ds(pl.multiple_of(me * share, share), share)

    pl.semaphore_wait(barrier, len(neighbours) + cols - 1)

    def swap(k):
        return pltpu.make_async_remote_copy(
            src_ref=x_ref.at[others_col[k]],
            dst_ref=buf.at[col, own_rows],
            send_sem=swap_send.at[k],
            recv_sem=swap_recv.at[col],
            device_id={"col": others_col[k]},
            device_id_type=MESH,
        )

    for k in range(last):
        swap(k).start()
    own = pltpu.make_async_copy(x_ref.at[col], buf.at[col, own_rows], own_sem.at[0])
    own.start()
    own.wait()

    drains = []

    def spread(turn, piece, before=None):
        def send(slot, device, relayed, oa, ob, h):
            pltpu.make_async_remote_copy(
                src_ref=slot,
                dst_ref=slot,
                send_sem=send_sem.at[len(drains)],
                recv_sem=recv_sem.at[turn, relayed, oa * 2 + ob, h],
                device_id={"tile": device},
                device_id_type=MESH,
            ).start()
            drains.append(piece)

        def arrived(relayed, oa, ob, h):
            slot = piece(oa, ob, h, 1 - core if relayed else core)
            pltpu.make_async_remote_copy(
                src_ref=slot,
                dst_ref=slot,
                send_sem=send_sem.at[0],
                recv_sem=recv_sem.at[turn, relayed, oa * 2 + ob, h],
                device_id={"tile": partner},
                device_id_type=MESH,
            ).wait_recv()

        def relay(oa, ob, h):
            send(piece(oa, ob, h, core), partner, 1, oa, ob, h)

        def forward(oa, ob, h, device, new_oa, new_ob):
            send(piece(oa, ob, h, core), device, 0, new_oa, new_ob, h)

        if before is not None:
            before()
        for h in (1, 0):
            forward(0, 0, h, device_at(0, 1), 0, 1)
        for h in (0, 1):
            for o in others:
                forward(0, 0, h, device_at(o, 0), (a_size - o) % a_size, 0)
        for h in (0, 1):
            relay(0, 0, h)
        yield
        arrived(0, 0, 1, 1)
        for o in others:
            forward(0, 1, 1, device_at(o, 0), (a_size - o) % a_size, 1)
        for o in others:
            arrived(0, o, 0, 0)
            forward(o, 0, 0, device_at(0, 1), o, 1)
        relay(0, 1, 1)
        for o in others:
            relay(o, 0, 0)
        yield
        arrived(0, 0, 1, 0)
        relay(0, 1, 0)
        for o in others:
            arrived(0, o, 0, 1)
            relay(o, 0, 1)
        for h in (0, 1):
            for o in others:
                arrived(0, o, 1, h)
                relay(o, 1, h)
        for h in (0, 1):
            arrived(1, 0, 0, h)
        for h in (1, 0):
            arrived(1, 0, 1, h)
        for o in others:
            for h in (0, 1):
                arrived(1, o, 0, h)
        for o in others:
            for h in (0, 1):
                arrived(1, o, 1, h)
        yield

    def gather(k):
        g = order[k]
        half = share // 2

        def piece(oa, ob, h, owner_core):
            start = (chip_at(oa, ob) * 2 + owner_core) * share + h * half
            return buf.at[g, pl.ds(pl.multiple_of(start, half), half)]

        def before():
            @pl.when(g != col)
            def _():
                slot = buf.at[g, own_rows]
                pltpu.make_async_remote_copy(
                    src_ref=slot,
                    dst_ref=slot,
                    send_sem=swap_send.at[0],
                    recv_sem=swap_recv.at[g],
                    device_id={"col": lax.rem(col + 1, cols)},
                    device_id_type=MESH,
                ).wait_recv()

        return spread(k, piece, before)

    def share_part(p, low, high):
        half = (high - low) * height // 2

        def piece(oa, ob, h, owner_core):
            start = (chip_at(oa, ob) * 2 + owner_core) * rows + low * height + h * half
            return whole.at[pl.ds(pl.multiple_of(start, half), half)]

        return spread(cols + p, piece)

    def pass_on(g, i):
        below = jnp.logical_and(g < col, g == col - 1)
        slot = jnp.where(below, cols, g)
        return pltpu.make_async_remote_copy(
            src_ref=sums.at[g, at(i)],
            dst_ref=sums.at[slot, at(i)],
            send_sem=sum_send.at[g, i],
            recv_sem=sum_recv.at[slot, i],
            device_id={"col": jnp.where(g > col, col + 1, col - 1)},
            device_id_type=MESH,
        )

    def passed(slot, i):
        pltpu.make_async_remote_copy(
            src_ref=sums.at[slot, at(i)],
            dst_ref=sums.at[slot, at(i)],
            send_sem=sum_send.at[0, 0],
            recv_sem=sum_recv.at[slot, i],
            device_id={"col": lax.rem(col + 1, cols)},
            device_id_type=MESH,
        ).wait_recv()

    lag = 2
    rising = 2 * col < cols

    def flow(up, turn, i):
        g = jnp.where(up, turn, last - turn)
        due = jnp.where(up, g - col, col - g) > 0

        @pl.when(due)
        def _():
            passed(g, i)
            sums[g, at(i), :] = (sums[g, at(i), :].astype(F32) + part[g, at(i), :]).astype(BF16)
            pass_on(g, i).start()

    def multiply(k, t):
        g = order_at(k)
        ends = jnp.logical_and(edge, g != col)

        @pl.when(k == 0)
        def _():
            fetch(t).wait()

        slot = lax.rem(t, slots)
        x = buf[g]
        a = jnp.dot(z_buf[slot, 0], x, preferred_element_type=F32)
        b = jnp.dot(z_buf[slot, 1], x, preferred_element_type=F32)
        term = jnp.concatenate([a[:, :lanes] - b[:, lanes:], a[:, lanes:] + b[:, :lanes]], 1)

        @pl.when(ends)
        def _():
            sums[g, tall(t), :] = term.astype(BF16)

            @pl.loop(0, each)
            def _(n):
                pass_on(g, t * each + n).start()

        @pl.when(jnp.logical_not(ends))
        def _():
            part[g, tall(t), :] = term

        if cols > 2:

            @pl.when(jnp.logical_and(inner, k == last))
            def _():
                @pl.loop(0, each)
                def _(n):
                    flow(rising, 2, t * each + n)
                    flow(jnp.logical_not(rising), 2, t * each + n)

    def forwards(low, high):
        first, count = low * each, (high - low) * each

        @pl.when(inner)
        def _():
            for turn in range(3, cols):

                @pl.loop(0, count + lag)
                def _(i):
                    @pl.when(i < count)
                    def _():
                        flow(rising, turn, first + i)

                    @pl.when(i >= lag)
                    def _():
                        flow(jnp.logical_not(rising), turn, first + i - lag)

    def finish(low, high):
        @pl.loop(low * each, high * each)
        def _(i):
            @pl.when(col > 0)
            def _():
                passed(col, i)
                part[col, at(i), :] += sums[col, at(i), :].astype(F32)

            @pl.when(col < last)
            def _():
                passed(cols, i)
                part[col, at(i), :] += sums[cols, at(i), :].astype(F32)

            total = part[col, at(i), :]
            pair = jnp.stack([total[:, :lanes], total[:, lanes:]], 1).astype(BF16)
            whole[pl.ds(pl.multiple_of(me * rows + i * block, block), block)] = pair

    stages = [gather(k) for k in range(cols)]

    def advance(k):
        if k < cols:
            next(stages[k])

    advance(0)
    advance(0)
    advance(1)
    advance(0)

    @pl.loop(0, 2 * cols)
    def _(n):
        for k in range(cols):

            @pl.when(n == 2 * k + 1)
            def _():
                advance(k + 1)
                advance(k + 2)

            @pl.when(n == 2 * k + 2)
            def _():
                advance(k + 1)

        multiply(n // 2, lax.rem(n, 2))

    fetch(3).start()
    parts = [share_part(0, 0, 2), share_part(1, 2, 3), share_part(2, 3, 4)]

    forwards(0, 2)

    @pl.loop(0, cols)
    def _(k):
        multiply(k, 2)

    finish(0, 2)
    next(parts[0])
    forwards(2, 3)

    @pl.loop(0, cols)
    def _(k):
        multiply(k, 3)

    next(parts[0])
    finish(2, 3)
    next(parts[1])
    next(parts[0])
    forwards(3, 4)
    finish(3, 4)
    mine = pltpu.make_async_copy(
        whole.at[pl.ds(pl.multiple_of(me * rows, rows), rows)], own_ref, own_sem.at[0]
    )
    mine.start()
    next(parts[1])
    next(parts[2])
    next(parts[1])
    next(parts[2])
    next(parts[2])
    step = 32

    @pl.loop(0, out_ref.shape[0] // step)
    def _(n):
        base = n * step
        for k in range(step):
            out_ref[base + k] = whole[index_ref[base + k]]

    mine.wait()
    for g in others_col:

        @pl.loop(0, blocks)
        def _(i):
            pass_on(g, i).wait_send()

    for k in range(last):
        swap(k).wait_send()
    for n, piece in enumerate(drains):
        slot = piece(0, 0, 0, core)
        pltpu.make_async_remote_copy(
            src_ref=slot,
            dst_ref=slot,
            send_sem=send_sem.at[n],
            recv_sem=recv_sem.at[0, 0, 0, 0],
            device_id={"tile": partner},
            device_id_type=MESH,
        ).wait_send()


def couple(index, impedance, x, tiles):
    _, rows, depth = impedance.shape
    cols, share, width = x.shape
    a_size = tiles // 4
    height = rows // 4
    blocks = 16
    lanes = width // 2
    copies = (cols + 3) * (2 + 2 * (a_size - 1) + 2 * (a_size - 1) + 2 * 2 * a_size)
    return pl.pallas_call(
        functools.partial(couple_kernel, tiles, cols),
        out_shape=(
            jax.ShapeDtypeStruct((index.shape[0], 2, lanes), BF16),
            jax.ShapeDtypeStruct((rows, 2, lanes), BF16),
        ),
        in_specs=[
            pl.BlockSpec(memory_space=pltpu.SMEM),
            pl.BlockSpec(memory_space=pl.ANY),
            pl.BlockSpec(memory_space=pltpu.VMEM),
        ],
        out_specs=(pl.BlockSpec(memory_space=pltpu.VMEM), pl.BlockSpec(memory_space=pltpu.VMEM)),
        scratch_shapes=[
            pltpu.VMEM((3, 2, height, depth), BF16),
            pltpu.SemaphoreType.DMA((4,)),
            pltpu.VMEM((cols, depth, width), BF16),
            pltpu.VMEM((cols, rows, width), F32),
            pltpu.VMEM((cols + 1, rows, width), BF16),
            pltpu.VMEM((tiles * rows, 2, lanes), BF16),
            pltpu.SemaphoreType.DMA((max(cols - 1, 1),)),
            pltpu.SemaphoreType.DMA((cols,)),
            pltpu.SemaphoreType.DMA((1,)),
            pltpu.SemaphoreType.DMA((copies,)),
            pltpu.SemaphoreType.DMA((cols + 3, 2, 2 * a_size, 2)),
            pltpu.SemaphoreType.DMA((cols, blocks)),
            pltpu.SemaphoreType.DMA((cols + 1, blocks)),
        ],
        compiler_params=pltpu.CompilerParams(
            collective_id=1, has_side_effects=True, vmem_limit_bytes=60 * 2**20
        ),
    )(index, impedance, x)


def places_of(sigma, tile, cols, tiles):
    count = sigma.shape[0]
    per = count // cols // tiles // LANES
    where = jnp.arange(count, dtype=jnp.int32)
    col = jnp.arange(cols, dtype=jnp.int32)[:, None]
    heads = ((col * tiles + tile) * per + jnp.arange(per, dtype=jnp.int32)[None, :]).reshape(-1)
    high = (sigma // LANES)[None, :] == heads[:, None]
    low = (sigma % LANES)[None, :] == jnp.arange(LANES, dtype=jnp.int32)[:, None]
    digits = jnp.stack([where // LANES, where % LANES])
    left = jnp.where(high[None], digits[:, None, :], 0).astype(BF16).reshape(-1, count)
    found = lax.dot_general(
        left, low.astype(BF16), (((1,), (1,)), ((), ())), preferred_element_type=F32
    ).reshape(2, -1)
    return (found[0] * LANES + found[1]).astype(jnp.int32)


def per_device(impedance, mobility, force, patch_map, ownership):
    slots, width, _ = mobility.shape
    patches = patch_map.shape[0]
    loads = force.shape[0]
    tiles = lax.axis_size("tile")
    cols = lax.axis_size("col")
    share = patches // cols // tiles
    mine = slots * width
    tile = lax.axis_index("tile")

    panels = patch_map.reshape(-1, width)
    slot_flat = panels[ownership].reshape(mine)
    owners = lax.all_gather(ownership, "tile", axis=0, tiled=True)
    share_index = places_of(panels[owners].reshape(patches), tile, cols, tiles)

    mob_re = mobility[:, :, :width]
    mob_im = mobility[:, :, width:]
    plain = jnp.concatenate(
        [jnp.concatenate([mob_re, -mob_im], 2), jnp.concatenate([mob_im, mob_re], 2)], 1
    )
    entry = jnp.arange(2 * width, dtype=jnp.int32)
    mixed = (entry % 2) * width + entry // 2
    mix = (mixed[:, None] == entry[None, :]).astype(BF16)

    def product(a, a_dim, b, b_dim, a_batch=0, b_batch=0):
        return lax.dot_general(a, b, (((a_dim,), (b_dim,)), ((a_batch,), (b_batch,))), preferred_element_type=F32)

    def rows_mixed(a):
        many = jnp.broadcast_to(mix, (slots,) + mix.shape)
        return product(many, 2, a, 1).astype(BF16)

    by_pair = lax.dot_general(plain, mix, (((2,), (1,)), ((), ())), preferred_element_type=F32).astype(BF16)
    pair_force = rows_mixed(plain)
    pair_pair = rows_mixed(by_pair)
    first = product(pair_force, 2, force, 2, 0, 1)
    first_out = product(force, 2, plain, 2, 1, 0)

    velocity = first.astype(BF16)
    for turn in range(ITERS):
        picked = gather_and_pick(share_index, velocity.reshape(mine, 2, loads), tiles)
        at_slots, pressure = couple(slot_flat, impedance, picked.reshape(cols, share, 2 * loads), tiles)
        at_slots = at_slots.reshape(slots, 2 * width, loads)
        if turn < ITERS - 1:
            velocity = (first - product(pair_pair, 2, at_slots, 1)).astype(BF16)
    velocity_out = (first_out - product(at_slots, 1, by_pair, 2)).astype(BF16).transpose(1, 0, 2)
    pressure_out = pressure.transpose(2, 1, 0)
    return velocity_out, pressure_out


def solution(mesh):
    return jax.shard_map(
        per_device,
        mesh=mesh,
        in_specs=(
            P(None, "tile", "col"),
            P("tile", None, None),
            P("col", "tile", None),
            P(),
            P("tile"),
        ),
        out_specs=(P("col", "tile", None), P("col", None, "tile")),
        check_vma=False,
    )
```

```python
import functools

import jax
import jax.numpy as jnp
from jax import lax
from jax.experimental import pallas as pl
from jax.experimental.pallas import tpu as pltpu
from jax.sharding import PartitionSpec as P

ITERS = 2
LANES = 128
BF16 = jnp.bfloat16
F32 = jnp.float32


MESH = pl.DeviceIdType.MESH


def gather_over_tile(tiles, x_ref, buf, send_sem, recv_sem, own_sem):
    a_size = tiles // 4
    rows = x_ref.shape[0]
    half = rows // 2
    me = lax.axis_index("tile")
    core = lax.rem(me, 2)
    my_b = lax.rem(me // 2, 2)
    my_a = me // 4
    others = range(1, a_size)

    def chip_at(oa, ob):
        return lax.rem(my_a + oa, a_size) * 2 + lax.rem(my_b + ob, 2)

    def device_at(oa, ob):
        return chip_at(oa, ob) * 2 + core

    partner = chip_at(0, 0) * 2 + 1 - core
    neighbours = [partner, device_at(0, 1)] + [device_at(o, 0) for o in others]

    barrier = pltpu.get_barrier_semaphore()
    for device in neighbours:
        pl.semaphore_signal(barrier, inc=1, device_id={"tile": device}, device_id_type=MESH)
    pl.semaphore_wait(barrier, len(neighbours))

    def piece(oa, ob, h, owner_core):
        start = (chip_at(oa, ob) * 2 + owner_core) * rows + h * half
        return buf.at[pl.ds(pl.multiple_of(start, half), half)]

    sent = []

    def send(src, dst, device, relayed, oa, ob, h):
        copy = pltpu.make_async_remote_copy(
            src_ref=src,
            dst_ref=dst,
            send_sem=send_sem.at[len(sent)],
            recv_sem=recv_sem.at[relayed, oa * 2 + ob, h],
            device_id={"tile": device},
            device_id_type=MESH,
        )
        copy.start()
        sent.append(copy)

    def arrived(relayed, oa, ob, h):
        slot = piece(oa, ob, h, 1 - core if relayed else core)
        pltpu.make_async_remote_copy(
            src_ref=slot,
            dst_ref=slot,
            send_sem=send_sem.at[0],
            recv_sem=recv_sem.at[relayed, oa * 2 + ob, h],
            device_id={"tile": partner},
            device_id_type=MESH,
        ).wait_recv()

    def relay(oa, ob, h):
        slot = piece(oa, ob, h, core)
        send(slot, slot, partner, 1, oa, ob, h)

    def forward(oa, ob, h, device, new_oa, new_ob):
        slot = piece(oa, ob, h, core)
        send(slot, slot, device, 0, new_oa, new_ob, h)

    def own(h):
        return x_ref.at[pl.ds(h * half, half)]

    for h in (1, 0):
        send(own(h), piece(0, 0, h, core), device_at(0, 1), 0, 0, 1, h)
    for h in (0, 1):
        for o in others:
            send(own(h), piece(0, 0, h, core), device_at(o, 0), 0, (a_size - o) % a_size, 0, h)
    for h in (0, 1):
        send(own(h), piece(0, 0, h, core), partner, 1, 0, 0, h)
    local = pltpu.make_async_copy(
        x_ref, buf.at[pl.ds(pl.multiple_of(me * rows, rows), rows)], own_sem.at[0]
    )
    local.start()
    local.wait()
    for h in (0, 1):
        arrived(1, 0, 0, h)

    arrived(0, 0, 1, 1)
    for o in others:
        forward(0, 1, 1, device_at(o, 0), (a_size - o) % a_size, 1)
    for o in others:
        arrived(0, o, 0, 0)
        forward(o, 0, 0, device_at(0, 1), o, 1)
    relay(0, 1, 1)
    for o in others:
        relay(o, 0, 0)
    arrived(0, 0, 1, 0)
    relay(0, 1, 0)
    for o in others:
        arrived(0, o, 0, 1)
        relay(o, 0, 1)
    for h in (1, 0):
        arrived(1, 0, 1, h)
    for o in others:
        for h in (0, 1):
            arrived(0, o, 1, h)
            relay(o, 1, h)
    for o in others:
        for h in (0, 1):
            arrived(1, o, 0, h)
    for o in others:
        for h in (0, 1):
            arrived(1, o, 1, h)
    for copy in sent:
        copy.wait_send()


def gather_scratch(tiles, shape):
    a_size = tiles // 4
    copies = 2 + 2 * (a_size - 1) + 2 * (a_size - 1) + 2 * 2 * a_size
    return [
        pltpu.VMEM((tiles * shape[0],) + shape[1:], BF16),
        pltpu.SemaphoreType.DMA((copies,)),
        pltpu.SemaphoreType.DMA((2, 2 * a_size, 2)),
        pltpu.SemaphoreType.DMA((1,)),
    ]


def pick_kernel(tiles, index_ref, x_ref, out_ref, buf, send_sem, recv_sem, own_sem):
    gather_over_tile(tiles, x_ref, buf, send_sem, recv_sem, own_sem)
    count = out_ref.shape[0]
    step = 32

    @pl.loop(0, count // step)
    def _(block):
        base = block * step
        for k in range(step):
            out_ref[base + k] = buf[index_ref[base + k]]


def gather_and_pick(index, rows, tiles):
    return pl.pallas_call(
        functools.partial(pick_kernel, tiles),
        out_shape=jax.ShapeDtypeStruct((index.shape[0],) + rows.shape[1:], rows.dtype),
        in_specs=[
            pl.BlockSpec(memory_space=pltpu.SMEM),
            pl.BlockSpec(memory_space=pltpu.VMEM),
        ],
        out_specs=pl.BlockSpec(memory_space=pltpu.VMEM),
        scratch_shapes=gather_scratch(tiles, rows.shape),
        compiler_params=pltpu.CompilerParams(
            collective_id=0, has_side_effects=True, vmem_limit_bytes=40 * 2**20
        ),
    )(index, rows)


def couple_kernel(
    tiles,
    cols,
    index_ref,
    z_ref,
    x_ref,
    out_ref,
    own_ref,
    z_buf,
    z_sem,
    buf,
    part,
    sums,
    whole,
    swap_send,
    swap_recv,
    own_sem,
    send_sem,
    recv_sem,
    sum_send,
    sum_recv,
):
    a_size = tiles // 4
    rows, _, lanes = own_ref.shape
    share = x_ref.shape[1]
    height = rows // 4
    each = 4
    block = height // each
    blocks = rows // block
    slots = z_buf.shape[0]
    col = lax.axis_index("col")
    me = lax.axis_index("tile")
    core = lax.rem(me, 2)
    my_b = lax.rem(me // 2, 2)
    my_a = me // 4
    others = range(1, a_size)

    def chip_at(oa, ob):
        return lax.rem(my_a + oa, a_size) * 2 + lax.rem(my_b + ob, 2)

    def device_at(oa, ob):
        return chip_at(oa, ob) * 2 + core

    partner = chip_at(0, 0) * 2 + 1 - core
    neighbours = [partner, device_at(0, 1)] + [device_at(o, 0) for o in others]

    barrier = pltpu.get_barrier_semaphore()
    for device in neighbours:
        pl.semaphore_signal(barrier, inc=1, device_id={"tile": device}, device_id_type=MESH)
    for o in range(1, cols):
        pl.semaphore_signal(barrier, inc=1, device_id={"col": lax.rem(col + o, cols)}, device_id_type=MESH)

    def at(i):
        return pl.ds(pl.multiple_of(i * block, block), block)

    def tall(t):
        return pl.ds(pl.multiple_of(t * height, height), height)

    def fetch(t):
        slot = lax.rem(t, slots)
        return pltpu.make_async_copy(z_ref.at[:, tall(t)], z_buf.at[slot], z_sem.at[t])

    for t in range(3):
        fetch(t).start()

    last = cols - 1
    edge = jnp.logical_or(col == 0, col == last)
    inner = jnp.logical_not(edge)
    near = jnp.minimum(col, last - col)

    def group(k):
        side = col + (k + 1) // 2 if k % 2 else col - k // 2
        rest = jnp.where(near == col, k, last - k)
        return jnp.where(k <= 2 * near, side, rest)

    others_col = [group(k) for k in range(1, cols)]
    order = [jnp.where(edge, a, b) for a, b in zip(others_col + [col], [col] + others_col)]

    def order_at(k):
        g = order[0]
        for n in range(1, cols):
            g = jnp.where(k == n, order[n], g)
        return g

    own_rows = pl.ds(pl.multiple_of(me * share, share), share)

    pl.semaphore_wait(barrier, len(neighbours) + cols - 1)

    def swap(k):
        return pltpu.make_async_remote_copy(
            src_ref=x_ref.at[others_col[k]],
            dst_ref=buf.at[col, own_rows],
            send_sem=swap_send.at[k],
            recv_sem=swap_recv.at[col],
            device_id={"col": others_col[k]},
            device_id_type=MESH,
        )

    for k in range(last):
        swap(k).start()
    own = pltpu.make_async_copy(x_ref.at[col], buf.at[col, own_rows], own_sem.at[0])
    own.start()
    own.wait()

    drains = []

    def spread(turn, piece, before=None):
        def send(slot, device, relayed, oa, ob, h):
            pltpu.make_async_remote_copy(
                src_ref=slot,
                dst_ref=slot,
                send_sem=send_sem.at[len(drains)],
                recv_sem=recv_sem.at[turn, relayed, oa * 2 + ob, h],
                device_id={"tile": device},
                device_id_type=MESH,
            ).start()
            drains.append(piece)

        def arrived(relayed, oa, ob, h):
            slot = piece(oa, ob, h, 1 - core if relayed else core)
            pltpu.make_async_remote_copy(
                src_ref=slot,
                dst_ref=slot,
                send_sem=send_sem.at[0],
                recv_sem=recv_sem.at[turn, relayed, oa * 2 + ob, h],
                device_id={"tile": partner},
                device_id_type=MESH,
            ).wait_recv()

        def relay(oa, ob, h):
            send(piece(oa, ob, h, core), partner, 1, oa, ob, h)

        def forward(oa, ob, h, device, new_oa, new_ob):
            send(piece(oa, ob, h, core), device, 0, new_oa, new_ob, h)

        if before is not None:
            before()
        for h in (1, 0):
            forward(0, 0, h, device_at(0, 1), 0, 1)
        for h in (0, 1):
            for o in others:
                forward(0, 0, h, device_at(o, 0), (a_size - o) % a_size, 0)
        for h in (0, 1):
            relay(0, 0, h)
        yield
        arrived(0, 0, 1, 1)
        for o in others:
            forward(0, 1, 1, device_at(o, 0), (a_size - o) % a_size, 1)
        for o in others:
            arrived(0, o, 0, 0)
            forward(o, 0, 0, device_at(0, 1), o, 1)
        relay(0, 1, 1)
        for o in others:
            relay(o, 0, 0)
        yield
        arrived(0, 0, 1, 0)
        relay(0, 1, 0)
        for o in others:
            arrived(0, o, 0, 1)
            relay(o, 0, 1)
        for h in (0, 1):
            for o in others:
                arrived(0, o, 1, h)
                relay(o, 1, h)
        for h in (0, 1):
            arrived(1, 0, 0, h)
        for h in (1, 0):
            arrived(1, 0, 1, h)
        for o in others:
            for h in (0, 1):
                arrived(1, o, 0, h)
        for o in others:
            for h in (0, 1):
                arrived(1, o, 1, h)
        yield

    def gather(k):
        g = order[k]
        half = share // 2

        def piece(oa, ob, h, owner_core):
            start = (chip_at(oa, ob) * 2 + owner_core) * share + h * half
            return buf.at[g, pl.ds(pl.multiple_of(start, half), half)]

        def before():
            @pl.when(g != col)
            def _():
                slot = buf.at[g, own_rows]
                pltpu.make_async_remote_copy(
                    src_ref=slot,
                    dst_ref=slot,
                    send_sem=swap_send.at[0],
                    recv_sem=swap_recv.at[g],
                    device_id={"col": lax.rem(col + 1, cols)},
                    device_id_type=MESH,
                ).wait_recv()

        return spread(k, piece, before)

    def share_part(p, low, high):
        half = (high - low) * height // 2

        def piece(oa, ob, h, owner_core):
            start = (chip_at(oa, ob) * 2 + owner_core) * rows + low * height + h * half
            return whole.at[pl.ds(pl.multiple_of(start, half), half)]

        return spread(cols + p, piece)

    def pass_on(g, i):
        below = jnp.logical_and(g < col, g == col - 1)
        slot = jnp.where(below, cols, g)
        return pltpu.make_async_remote_copy(
            src_ref=sums.at[g, at(i)],
            dst_ref=sums.at[slot, at(i)],
            send_sem=sum_send.at[g, i],
            recv_sem=sum_recv.at[slot, i],
            device_id={"col": jnp.where(g > col, col + 1, col - 1)},
            device_id_type=MESH,
        )

    def passed(slot, i):
        pltpu.make_async_remote_copy(
            src_ref=sums.at[slot, at(i)],
            dst_ref=sums.at[slot, at(i)],
            send_sem=sum_send.at[0, 0],
            recv_sem=sum_recv.at[slot, i],
            device_id={"col": lax.rem(col + 1, cols)},
            device_id_type=MESH,
        ).wait_recv()

    lag = 2
    rising = 2 * col < cols

    def flow(up, turn, i):
        g = jnp.where(up, turn, last - turn)
        due = jnp.where(up, g - col, col - g) > 0

        @pl.when(due)
        def _():
            passed(g, i)
            sums[g, at(i), :] = (sums[g, at(i), :].astype(F32) + part[g, at(i), :]).astype(BF16)
            pass_on(g, i).start()

    def multiply(k, t, passing):
        g = order_at(k)
        ends = jnp.logical_and(edge, g != col)

        @pl.when(k == 0)
        def _():
            fetch(t).wait()

        slot = lax.rem(t, slots)
        x = buf[g]
        a = jnp.dot(z_buf[slot, 0], x, preferred_element_type=F32)
        b = jnp.dot(z_buf[slot, 1], x, preferred_element_type=F32)
        term = jnp.concatenate([a[:, :lanes] - b[:, lanes:], a[:, lanes:] + b[:, :lanes]], 1)

        @pl.when(ends)
        def _():
            sums[g, tall(t), :] = term.astype(BF16)

            @pl.loop(0, each)
            def _(n):
                pass_on(g, t * each + n).start()

        @pl.when(jnp.logical_not(ends))
        def _():
            part[g, tall(t), :] = term

        if passing and cols > 2:

            @pl.when(jnp.logical_and(inner, k == last))
            def _():
                @pl.loop(0, each)
                def _(n):
                    flow(rising, 2, t * each + n)
                    flow(jnp.logical_not(rising), 2, t * each + n)

    def forwards(turns, low, high):
        first, count = low * each, (high - low) * each

        @pl.when(inner)
        def _():
            for turn in turns:

                @pl.loop(0, count + lag)
                def _(i):
                    @pl.when(i < count)
                    def _():
                        flow(rising, turn, first + i)

                    @pl.when(i >= lag)
                    def _():
                        flow(jnp.logical_not(rising), turn, first + i - lag)

    def finish(low, high):
        @pl.loop(low * each, high * each)
        def _(i):
            @pl.when(col > 0)
            def _():
                passed(col, i)
                part[col, at(i), :] += sums[col, at(i), :].astype(F32)

            @pl.when(col < last)
            def _():
                passed(cols, i)
                part[col, at(i), :] += sums[cols, at(i), :].astype(F32)

            total = part[col, at(i), :]
            pair = jnp.stack([total[:, :lanes], total[:, lanes:]], 1).astype(BF16)
            whole[pl.ds(pl.multiple_of(me * rows + i * block, block), block)] = pair

    stages = [gather(k) for k in range(cols)]

    def advance(k):
        if k < cols:
            next(stages[k])

    advance(0)
    advance(0)
    advance(1)
    advance(0)

    @pl.loop(0, 2 * cols)
    def _(n):
        for k in range(cols):

            @pl.when(n == 2 * k + 1)
            def _():
                advance(k + 1)
                advance(k + 2)

            @pl.when(n == 2 * k + 2)
            def _():
                advance(k + 1)

        multiply(n // 2, lax.rem(n, 2), True)

    fetch(3).start()
    parts = [share_part(0, 0, 2), share_part(1, 2, 3), share_part(2, 3, 4)]

    early, late = range(2, min(3, cols)), range(3, cols)

    @pl.loop(0, cols)
    def _(k):
        multiply(k, 2, False)

    forwards(late, 0, 2)
    finish(0, 2)
    next(parts[0])

    @pl.loop(0, cols)
    def _(k):
        multiply(k, 3, False)

    forwards(early, 2, 3)
    next(parts[0])
    forwards(late, 2, 3)
    finish(2, 3)
    next(parts[1])
    forwards(early, 3, 4)
    next(parts[0])
    next(parts[1])
    forwards(late, 3, 4)
    finish(3, 4)
    mine = pltpu.make_async_copy(
        whole.at[pl.ds(pl.multiple_of(me * rows, rows), rows)], own_ref, own_sem.at[0]
    )
    mine.start()
    next(parts[2])
    next(parts[1])
    next(parts[2])
    next(parts[2])
    step = 32

    @pl.loop(0, out_ref.shape[0] // step)
    def _(n):
        base = n * step
        for k in range(step):
            out_ref[base + k] = whole[index_ref[base + k]]

    mine.wait()
    for g in others_col:

        @pl.loop(0, blocks)
        def _(i):
            pass_on(g, i).wait_send()

    for k in range(last):
        swap(k).wait_send()
    for n, piece in enumerate(drains):
        slot = piece(0, 0, 0, core)
        pltpu.make_async_remote_copy(
            src_ref=slot,
            dst_ref=slot,
            send_sem=send_sem.at[n],
            recv_sem=recv_sem.at[0, 0, 0, 0],
            device_id={"tile": partner},
            device_id_type=MESH,
        ).wait_send()


def couple(index, impedance, x, tiles):
    _, rows, depth = impedance.shape
    cols, share, width = x.shape
    a_size = tiles // 4
    height = rows // 4
    blocks = 16
    lanes = width // 2
    copies = (cols + 3) * (2 + 2 * (a_size - 1) + 2 * (a_size - 1) + 2 * 2 * a_size)
    return pl.pallas_call(
        functools.partial(couple_kernel, tiles, cols),
        out_shape=(
            jax.ShapeDtypeStruct((index.shape[0], 2, lanes), BF16),
            jax.ShapeDtypeStruct((rows, 2, lanes), BF16),
        ),
        in_specs=[
            pl.BlockSpec(memory_space=pltpu.SMEM),
            pl.BlockSpec(memory_space=pl.ANY),
            pl.BlockSpec(memory_space=pltpu.VMEM),
        ],
        out_specs=(pl.BlockSpec(memory_space=pltpu.VMEM), pl.BlockSpec(memory_space=pltpu.VMEM)),
        scratch_shapes=[
            pltpu.VMEM((3, 2, height, depth), BF16),
            pltpu.SemaphoreType.DMA((4,)),
            pltpu.VMEM((cols, depth, width), BF16),
            pltpu.VMEM((cols, rows, width), F32),
            pltpu.VMEM((cols + 1, rows, width), BF16),
            pltpu.VMEM((tiles * rows, 2, lanes), BF16),
            pltpu.SemaphoreType.DMA((max(cols - 1, 1),)),
            pltpu.SemaphoreType.DMA((cols,)),
            pltpu.SemaphoreType.DMA((1,)),
            pltpu.SemaphoreType.DMA((copies,)),
            pltpu.SemaphoreType.DMA((cols + 3, 2, 2 * a_size, 2)),
            pltpu.SemaphoreType.DMA((cols, blocks)),
            pltpu.SemaphoreType.DMA((cols + 1, blocks)),
        ],
        compiler_params=pltpu.CompilerParams(
            collective_id=1, has_side_effects=True, vmem_limit_bytes=60 * 2**20
        ),
    )(index, impedance, x)


def places_of(sigma, tile, cols, tiles):
    count = sigma.shape[0]
    per = count // cols // tiles // LANES
    where = jnp.arange(count, dtype=jnp.int32)
    col = jnp.arange(cols, dtype=jnp.int32)[:, None]
    heads = ((col * tiles + tile) * per + jnp.arange(per, dtype=jnp.int32)[None, :]).reshape(-1)
    high = (sigma // LANES)[None, :] == heads[:, None]
    low = (sigma % LANES)[None, :] == jnp.arange(LANES, dtype=jnp.int32)[:, None]
    digits = jnp.stack([where // LANES, where % LANES])
    left = jnp.where(high[None], digits[:, None, :], 0).astype(BF16).reshape(-1, count)
    found = lax.dot_general(
        left, low.astype(BF16), (((1,), (1,)), ((), ())), preferred_element_type=F32
    ).reshape(2, -1)
    return (found[0] * LANES + found[1]).astype(jnp.int32)


def per_device(impedance, mobility, force, patch_map, ownership):
    slots, width, _ = mobility.shape
    patches = patch_map.shape[0]
    loads = force.shape[0]
    tiles = lax.axis_size("tile")
    cols = lax.axis_size("col")
    share = patches // cols // tiles
    mine = slots * width
    tile = lax.axis_index("tile")

    panels = patch_map.reshape(-1, width)
    slot_flat = panels[ownership].reshape(mine)
    owners = lax.all_gather(ownership, "tile", axis=0, tiled=True)
    share_index = places_of(panels[owners].reshape(patches), tile, cols, tiles)

    mob_re = mobility[:, :, :width]
    mob_im = mobility[:, :, width:]
    plain = jnp.concatenate(
        [jnp.concatenate([mob_re, -mob_im], 2), jnp.concatenate([mob_im, mob_re], 2)], 1
    )
    entry = jnp.arange(2 * width, dtype=jnp.int32)
    mixed = (entry % 2) * width + entry // 2
    mix = (mixed[:, None] == entry[None, :]).astype(BF16)

    def product(a, a_dim, b, b_dim, a_batch=0, b_batch=0):
        return lax.dot_general(a, b, (((a_dim,), (b_dim,)), ((a_batch,), (b_batch,))), preferred_element_type=F32)

    def rows_mixed(a):
        many = jnp.broadcast_to(mix, (slots,) + mix.shape)
        return product(many, 2, a, 1).astype(BF16)

    by_pair = lax.dot_general(plain, mix, (((2,), (1,)), ((), ())), preferred_element_type=F32).astype(BF16)
    pair_force = rows_mixed(plain)
    pair_pair = rows_mixed(by_pair)
    first = product(pair_force, 2, force, 2, 0, 1)
    first_out = product(force, 2, plain, 2, 1, 0)

    velocity = first.astype(BF16)
    for turn in range(ITERS):
        picked = gather_and_pick(share_index, velocity.reshape(mine, 2, loads), tiles)
        at_slots, pressure = couple(slot_flat, impedance, picked.reshape(cols, share, 2 * loads), tiles)
        at_slots = at_slots.reshape(slots, 2 * width, loads)
        if turn < ITERS - 1:
            velocity = (first - product(pair_pair, 2, at_slots, 1)).astype(BF16)
    velocity_out = (first_out - product(at_slots, 1, by_pair, 2)).astype(BF16).transpose(1, 0, 2)
    pressure_out = pressure.transpose(2, 1, 0)
    return velocity_out, pressure_out


def solution(mesh):
    return jax.shard_map(
        per_device,
        mesh=mesh,
        in_specs=(
            P(None, "tile", "col"),
            P("tile", None, None),
            P("col", "tile", None),
            P(),
            P("tile"),
        ),
        out_specs=(P("col", "tile", None), P("col", None, "tile")),
        check_vma=False,
    )
```
